32 devices in a mesh: groups: 2 (over x), lon: 16 (over z, y, core).
Axes of the slice: x: 2, y: 2, z: 4, core: 2. Of those that a mesh axis runs over, the one named last changes fastest.
Arguments:
- scene: bfloat16 [4, 48, 128, 320], P('groups', None, 'lon'), parts along dimension 0, may hold values from -24 to 24
- grad_out: bfloat16 [4, 48, 128, 320], P('groups', None, 'lon'), parts along dimension 0, may hold values from -6 to 6
- conv_first: bfloat16 [3, 3, 320, 320], replicated, may hold values from -0.109375 to 0.109375
- conv_second: bfloat16 [3, 3, 320, 320], replicated, may hold values from -0.109375 to 0.109375
- gain_first: float32 [320], replicated, may hold values from 0.25 to 1.75
- shift_first: float32 [320], replicated, may hold values from -3 to 3
- gain_second: float32 [320], replicated, may hold values from 0.25 to 1.75
- shift_second: float32 [320], replicated, may hold values from -3 to 3
Outputs:
- grad_input: bfloat16 [4, 48, 128, 320], P('groups', None, 'lon'), parts along dimension 0
- grad_first: float32 [1843200], P(('groups', 'lon')), parts along dimension 0
- grad_second: float32 [1843200], P(('groups', 'lon')), parts along dimension 0
The draws below stay inside these ranges and needn't reach their ends.
There are 2 independent parts, one for each index of `groups`. The reference program is written for one: setup_inputs(seed, part) draws one part's arguments, and reference() takes and returns one part's arrays. A program takes and returns all parts, laid end to end along the dimension named above; an argument that names none is the same for every part. Nothing has to cross between parts.
All inputs are finite; a program needn't handle non-finite values.
Results may differ from the reference program's by a relative error of at most 0.0031.
Values may be sent and summed in bfloat16 or wider, within the bound.
A program may use at most 128 MiB of HBM per device.

```python
import jax
import jax.numpy as jnp
from jax import lax

C = 320
GROUPS = 32
SCENES = 2
ROWS = 48
COLS = 128


def draw_scene(key, part):
    shape = (SCENES, ROWS, COLS, C)
    first = jax.random.fold_in(key, 0)
    third = jax.random.fold_in(key, 2)
    phase = jax.random.uniform(third, (), jnp.float32, 0.0, 6.2831853)
    column = jnp.arange(COLS, dtype=jnp.float32) / COLS
    level = 0.5 + 0.5 * jnp.cos(6.2831853 * column + phase)
    scale = (0.25 * jnp.exp(level * 3.1780538))[None, None, :, None]
    values = jax.random.truncated_normal(first, -4.0, 4.0, shape, jnp.float32) * scale
    values = jnp.clip(values, -24.0, 24.0)
    return values.astype(jnp.bfloat16)


def draw_grad_out(key, part):
    shape = (SCENES, ROWS, COLS, C)
    first, second = jax.random.split(jax.random.fold_in(key, 17))
    base = jax.random.truncated_normal(first, -4.0, 4.0, shape, jnp.float32)
    bias = 0.5 * jax.random.truncated_normal(second, -3.0, 3.0, (SCENES, 1, 1, C), jnp.float32)
    values = base + bias
    return values.astype(jnp.bfloat16)


def gaussian(stream_key, shape, deviation, bound, held_as=jnp.bfloat16):
    entries = jax.random.normal(stream_key, shape, jnp.float32) * deviation
    return jnp.minimum(jnp.maximum(entries, -bound), bound).astype(held_as)


def setup_inputs(seed: int = 0, part: int = 0) -> dict:
    seeds = jax.random.split(jax.random.key(seed), 9)
    part_keys = jax.random.split(jax.random.fold_in(seeds[8], part), 9)
    return {
        "scene": draw_scene(jax.random.fold_in(jax.random.fold_in(seeds[8], part), 71), part),
        "grad_out": draw_grad_out(jax.random.fold_in(jax.random.fold_in(seeds[8], part), 71), part),
        "conv_first": gaussian(seeds[2], (3, 3, C, C), (9 * C) ** -0.5, 0.109375),
        "conv_second": gaussian(seeds[3], (3, 3, C, C), (9 * C) ** -0.5, 0.109375),
        "gain_first": jnp.clip(1.0 + 0.15 * jax.random.normal(seeds[4], (C,), jnp.float32), 0.25, 1.75),
        "shift_first": gaussian(seeds[5], (C,), 0.5, 3.0, jnp.float32),
        "gain_second": jnp.clip(1.0 + 0.15 * jax.random.normal(seeds[6], (C,), jnp.float32), 0.25, 1.75),
        "shift_second": gaussian(seeds[7], (C,), 0.5, 3.0, jnp.float32),
    }


def cycle_pad(v):
    wrapped = jnp.concatenate([v[:, :, -1:], v, v[:, :, :1]], axis=2)
    return jnp.pad(wrapped, ((0, 0), (1, 1), (0, 0), (0, 0)))

def patches_of(padded):
    height = padded.shape[1] - 2
    width = padded.shape[2] - 2
    taps = [padded[:, i:i + height, j:j + width, :] for i in range(3) for j in range(3)]
    joined = jnp.concatenate(taps, axis=-1)
    return joined.reshape(-1, joined.shape[-1])

def convolve(padded, kernel, shape):
    chans = kernel.shape[2]
    out = jnp.dot(patches_of(padded), kernel.reshape(9 * chans, -1), preferred_element_type=jnp.float32)
    return out.reshape(shape)

def flipped(kernel):
    return jnp.transpose(kernel[::-1, ::-1], (0, 1, 3, 2))

def group_view(v):
    return v.reshape(v.shape[0], v.shape[1], v.shape[2], GROUPS, -1)

def norm_forward(v, gain, shift):
    grouped = group_view(v)
    mean = lax.optimization_barrier(jnp.mean(grouped, axis=(1, 2, 4), keepdims=True))
    spread = lax.optimization_barrier(jnp.mean((grouped - mean) ** 2, axis=(1, 2, 4), keepdims=True))
    inverse = 1.0 / jnp.sqrt(spread + 1e-05)
    vhat = ((grouped - mean) * inverse).reshape(v.shape)
    return (vhat * gain + shift, vhat, inverse)

def norm_backward(dact, vhat, inverse, gain):
    delta = group_view(dact * gain)
    grouped = group_view(vhat)
    first = lax.optimization_barrier(jnp.mean(delta, axis=(1, 2, 4), keepdims=True))
    second = lax.optimization_barrier(jnp.mean(delta * grouped, axis=(1, 2, 4), keepdims=True))
    return ((delta - first - grouped * second) * inverse).reshape(dact.shape)

def silu_slope(a):
    sig = jax.nn.sigmoid(a)
    return sig * (1.0 + a * (1.0 - sig))

def reference(scene, grad_out, conv_first, conv_second, gain_first, shift_first, gain_second, shift_second):
    shape = scene.shape
    act_first, vhat_first, inv_first = norm_forward(scene.astype(jnp.float32), gain_first, shift_first)
    silu_first = jax.nn.silu(act_first).astype(jnp.bfloat16)
    pad_first = cycle_pad(silu_first)
    inner = convolve(pad_first, conv_first, shape)
    act_second, vhat_second, inv_second = norm_forward(inner, gain_second, shift_second)
    silu_second = jax.nn.silu(act_second).astype(jnp.bfloat16)
    flat_out = grad_out.reshape(-1, shape[-1])
    grad_second = jnp.dot(patches_of(cycle_pad(silu_second)).T, flat_out, preferred_element_type=jnp.float32)
    dsilu_second = convolve(cycle_pad(grad_out), flipped(conv_second), shape)
    dact_second = dsilu_second * silu_slope(act_second)
    dinner = norm_backward(dact_second, vhat_second, inv_second, gain_second).astype(jnp.bfloat16)
    grad_first = jnp.dot(patches_of(pad_first).T, dinner.reshape(-1, shape[-1]), preferred_element_type=jnp.float32)
    dsilu_first = convolve(cycle_pad(dinner), flipped(conv_first), shape)
    dact_first = dsilu_first * silu_slope(act_first)
    dscene = norm_backward(dact_first, vhat_first, inv_first, gain_first)
    grad_input = (grad_out.astype(jnp.float32) + dscene).astype(jnp.bfloat16)
    return (grad_input, grad_first.reshape(-1), grad_second.reshape(-1))
```

```python
import functools

import jax
import jax.numpy as jnp
from jax import lax
from jax.experimental import pallas as pl
from jax.experimental.pallas import tpu as pltpu
from jax.sharding import PartitionSpec as P

GROUPS = 32
F32 = jnp.float32
BF16 = jnp.bfloat16
MESH = pl.DeviceIdType.MESH
HIGH = lax.Precision.HIGHEST


def window(rows, n):
    if n % 2 or rows % n or (2 * rows // n) % 8:
        return None
    own = rows // n
    off = own // 8 * 8
    return own, off, 2 * own - off


def sigmoid(a):
    return 1.0 / (1.0 + jnp.exp(-a))


def slope(a):
    sig = sigmoid(a)
    return sig * (1.0 + a * (1.0 - sig))


def kernel(n, height, eps_count, win, *refs):
    (x_ref, g_ref, w1_ref, w2_ref, par_ref, mix_ref, out_ref, d1_ref, d2_ref) = refs[:9]
    (
        st_send, st_recv, ha_send, ha_recv, hb_send, hb_recv, hc_send, hc_recv,
        pad, vbuf, ubuf, gbuf, dbuf, inner, dsil, delta, dinn, coef, vh_halo,
        st_ss, st_rs, h_ss, h_rs,
    ) = refs[9:32]
    pixels, chans = x_ref.shape
    tile = 16 * (height // 3)
    tiles = pixels // tile
    edge_rows = pixels // 8
    me = lax.axis_index("lon")
    right, left = lax.rem(me + 1, n), lax.rem(me + n - 1, n)

    def at(t):
        return pl.ds(pl.multiple_of(t * tile, 16), tile)

    def greet(k, _):
        pl.semaphore_signal(
            barrier, inc=1, device_id={"lon": lax.rem(me + k, n)}, device_id_type=MESH
        )
        return 0

    barrier = pltpu.get_barrier_semaphore()
    lax.fori_loop(1, n, greet, 0)

    def stat_copy(rnd, k):
        return pltpu.make_async_remote_copy(
            src_ref=st_send.at[rnd],
            dst_ref=st_recv.at[rnd, k],
            send_sem=st_ss.at[rnd, k],
            recv_sem=st_rs.at[rnd, k],
            device_id={"lon": lax.rem(me + k, n)},
            device_id_type=MESH,
        )

    def stat_put(rnd, total, second):
        rows = [
            jnp.sum(v[8 * b : 8 * b + 8], axis=0, keepdims=True)
            for v in (total, second)
            for b in range(2)
        ]
        block = jnp.concatenate(rows + [jnp.zeros((4, chans), F32)], axis=0)
        st_send[rnd] = block
        st_recv[rnd, 0] = block

    def stat_start(rnd):
        def go(k, _):
            stat_copy(rnd, k).start()
            return 0

        lax.fori_loop(1, n, go, 0)

    def stat_end(rnd):
        def end(k, _):
            stat_copy(rnd, k).wait()
            return 0

        lax.fori_loop(1, n, end, 0)

        def add(k, acc):
            return acc + st_recv[rnd, k]

        total = lax.fori_loop(1, n, add, st_recv[rnd, 0])
        means = (
            jnp.dot(total, mix_ref[...], precision=HIGH, preferred_element_type=F32)
            * (1.0 / eps_count)
        )
        return [means[r : r + 1] for r in range(4)]

    def halo_copies(rnd, send, recv):
        return [
            pltpu.make_async_remote_copy(
                src_ref=send.at[side],
                dst_ref=recv.at[1 - side],
                send_sem=h_ss.at[rnd, side],
                recv_sem=h_rs.at[rnd, 1 - side],
                device_id={"lon": peer},
                device_id_type=MESH,
            )
            for side, peer in ((0, left), (1, right))
        ]

    def halo_end(rnd, send, recv):
        copies = halo_copies(rnd, send, recv)
        for copy in copies:
            copy.wait_send()
        for copy in copies:
            copy.wait_recv()

    def pick(column, dtype):
        r = lax.broadcasted_iota(jnp.int32, (edge_rows, pixels), 0)
        p = lax.broadcasted_iota(jnp.int32, (edge_rows, pixels), 1)
        return jnp.where(p == 8 * r + column, 1.0, 0.0).astype(dtype)

    def edge(value, column):
        if value.dtype == BF16:
            return jnp.dot(pick(column, BF16), value, preferred_element_type=F32).astype(BF16)
        return jnp.dot(pick(column, F32), value, precision=HIGH, preferred_element_type=F32)

    def both(first, second):
        return jnp.concatenate(
            [jnp.broadcast_to(first, (8, chans)), jnp.broadcast_to(second, (8, chans))], axis=0
        )

    def halo_both(first, second):
        odd = lax.broadcasted_iota(jnp.int32, (edge_rows, chans), 0) & 1
        return jnp.where(odd == 0, first, second)

    def split(v):
        return v.reshape(v.shape[0] // 16, 16, chans)

    def fold(v):
        return jnp.sum(split(v), axis=0)

    def shifts(buf, low, high):
        zero = jnp.zeros((16, chans), BF16)
        for j in range(3):
            buf[j, 0:16] = zero
            buf[j, pixels + 16 : pixels + 32] = zero
        column = lax.broadcasted_iota(jnp.int32, (tile, chans), 0) & 7
        for t in range(tiles):
            p = lax.broadcasted_iota(jnp.int32, (tile, edge_rows), 0) + t * tile
            r = lax.broadcasted_iota(jnp.int32, (tile, edge_rows), 1)
            place = jnp.where((p >> 3) == r, 1.0, 0.0).astype(BF16)
            start = t * tile
            rows = slice(16 + start, 16 + start + tile)
            from_low = jnp.dot(place, low, preferred_element_type=F32)
            from_high = jnp.dot(place, high, preferred_element_type=F32)
            buf[0, rows] = jnp.where(
                column == 0, from_low, pad[start + 7 : start + 7 + tile]
            ).astype(BF16)
            buf[1, rows] = pad[start + 8 : start + 8 + tile].astype(BF16)
            buf[2, rows] = jnp.where(
                column == 7, from_high, pad[start + 9 : start + 9 + tile]
            ).astype(BF16)

    def pad_at(t):
        return pl.ds(pl.multiple_of(t * tile + 8, 8), tile)

    def taps(buf, w_ref, t, transposed):
        acc = jnp.zeros((tile, chans), F32)
        for i in range(3):
            for j in range(3):
                rows = pl.ds(pl.multiple_of(t * tile + 16 * i, 16), tile)
                lhs = buf[j, rows, :]
                if transposed:
                    acc += lax.dot_general(
                        lhs, w_ref[8 - 3 * i - j], (((1,), (1,)), ((), ())),
                        preferred_element_type=F32,
                    )
                else:
                    acc += jnp.dot(lhs, w_ref[3 * i + j], preferred_element_type=F32)
        return acc

    def loop(body):
        def step(t, carry):
            body(t)
            return carry

        lax.fori_loop(0, tiles, step, 0)

    def loop_sums(body):
        zero = jnp.zeros((16, chans), F32)

        def step(t, carry):
            a, b = body(t)
            return carry[0] + a, carry[1] + b

        return lax.fori_loop(0, tiles, step, (zero, zero))

    gain1, shift1 = par_ref[0:1], par_ref[1:2]
    gain2, shift2 = par_ref[2:3], par_ref[3:4]

    def sums_x(t):
        v = x_ref[at(t), :].astype(F32)
        return fold(v), fold(v * v)

    stat_put(0, *loop_sums(sums_x))
    for side, column in ((0, 0), (1, 7)):
        ha_send[side, 0:edge_rows] = edge(x_ref[...], column)
        ha_send[side, edge_rows : 2 * edge_rows] = edge(g_ref[...], column)
    pad[0:8] = jnp.zeros((8, chans), F32)
    pad[pixels + 8 : pixels + 16] = jnp.zeros((8, chans), F32)
    pl.semaphore_wait(barrier, n - 1)
    stat_start(0)
    for copy in halo_copies(0, ha_send, ha_recv):
        copy.start()

    def pad_g(t):
        pad[pad_at(t), :] = g_ref[at(t), :].astype(F32)

    loop(pad_g)
    halo_end(0, ha_send, ha_recv)
    shifts(gbuf, ha_recv[0, edge_rows : 2 * edge_rows], ha_recv[1, edge_rows : 2 * edge_rows])

    def conv_g(t):
        dsil[at(t), :] = taps(gbuf, w2_ref, t, True)

    loop(conv_g)

    def norm_coefs(rnd):
        m0, m1, q0, q1 = stat_end(rnd)
        i0 = 1.0 / jnp.sqrt(q0 - m0 * m0 + 1e-05)
        i1 = 1.0 / jnp.sqrt(q1 - m1 * m1 + 1e-05)
        return m0, m1, i0, i1

    m0, m1, i0, i1 = norm_coefs(0)
    coef[0] = both(m0, m1)
    coef[1] = both(i0, i1)
    halo_m, halo_i = halo_both(m0, m1), halo_both(i0, i1)

    def vhat_first(t):
        v = split(x_ref[at(t), :].astype(F32))
        return (v - coef[0][None]) * coef[1][None]

    def act_first(t):
        return vhat_first(t).reshape(tile, chans) * gain1 + shift1

    def silu_first(t):
        a = act_first(t)
        pad[pad_at(t), :] = a * sigmoid(a)

    loop(silu_first)
    sides = []
    for side in range(2):
        a = (ha_recv[side, 0:edge_rows].astype(F32) - halo_m) * halo_i * gain1 + shift1
        sides.append((a * sigmoid(a)).astype(BF16))
    shifts(vbuf, *sides)

    def conv_x(t):
        v = taps(vbuf, w1_ref, t, False)
        inner[at(t), :] = v
        return fold(v), fold(v * v)

    stat_put(1, *loop_sums(conv_x))
    stat_start(1)
    hb_send[0] = edge(inner[...], 0)
    hb_send[1] = edge(inner[...], 7)
    for copy in halo_copies(1, hb_send, hb_recv):
        copy.start()

    m0, m1, i0, i1 = norm_coefs(1)
    coef[2] = both(m0, m1)
    coef[3] = both(i0, i1)
    halo_m, halo_i = halo_both(m0, m1), halo_both(i0, i1)

    def second(t):
        vhat = ((split(inner[at(t), :]) - coef[2][None]) * coef[3][None]).reshape(tile, chans)
        inner[at(t), :] = vhat
        a = vhat * gain2 + shift2
        pad[pad_at(t), :] = a * sigmoid(a)
        d = dsil[at(t), :] * slope(a) * gain2
        delta[at(t), :] = d
        return fold(d), fold(d * vhat)

    stat_put(2, *loop_sums(second))
    stat_start(2)
    hc_send[0] = edge(delta[...], 0)
    hc_send[1] = edge(delta[...], 7)
    for copy in halo_copies(2, hc_send, hc_recv):
        copy.start()

    halo_end(1, hb_send, hb_recv)
    sides = []
    for side in range(2):
        vhat = (hb_recv[side] - halo_m) * halo_i
        vh_halo[side] = vhat
        a = vhat * gain2 + shift2
        sides.append((a * sigmoid(a)).astype(BF16))
    shifts(ubuf, *sides)

    def weight_gradient(buf, y, store):
        for i in range(3):
            for j in range(3):
                block = lax.dot_general(
                    buf[j, 16 * i : 16 * i + pixels], y, (((0,), (0,)), ((), ())),
                    preferred_element_type=F32,
                )
                store(3 * i + j, block)

    if win is None:

        def put(ref):
            def store(tap, block):
                ref[tap] = block

            return store

        weight_gradient(ubuf, g_ref[...], put(d2_ref))
    else:
        (full, core_in, chip_out, chip_in, c_ss, c_rs, q_ss, q_rs) = refs[32:]
        own, off, length = win
        chips = n // 2
        chip, core = me // 2, lax.rem(me, 2)
        mine = pl.ds(pl.multiple_of(off * core, 8), length)
        other = pl.ds(pl.multiple_of(off * (1 - core), 8), length)

        def put(slot):
            def store(tap, block):
                row = tap * chans
                while row < (tap + 1) * chans:
                    q, r = divmod(row, 2 * own)
                    stop = min((tap + 1) * chans, (q + 1) * 2 * own)
                    low = row - tap * chans
                    full[slot, q, r : r + stop - row] = block[low : low + stop - row]
                    row = stop

            return store

        def core_copy(slot):
            return pltpu.make_async_remote_copy(
                src_ref=full.at[slot, :, other, :],
                dst_ref=core_in.at[slot],
                send_sem=c_ss.at[slot],
                recv_sem=c_rs.at[slot],
                device_id={"lon": me + 1 - 2 * core},
                device_id_type=MESH,
            )

        def chip_copy(slot, k):
            to = lax.rem(chip + k, chips)
            return pltpu.make_async_remote_copy(
                src_ref=chip_out.at[slot, to],
                dst_ref=chip_in.at[slot, k],
                send_sem=q_ss.at[slot, k],
                recv_sem=q_rs.at[slot, k],
                device_id={"lon": 2 * to + core},
                device_id_type=MESH,
            )

        def chip_start(slot):
            core_copy(slot).wait()

            def go(k, _):
                to = lax.rem(chip + k, chips)
                chip_out[slot, to] = (full[slot, to, mine, :] + core_in[slot, to]).astype(BF16)
                chip_copy(slot, k).start()
                return 0

            lax.fori_loop(1, chips, go, 0)

        def chip_end(slot, ref):
            def end(k, _):
                chip_copy(slot, k).wait()
                return 0

            lax.fori_loop(1, chips, end, 0)

            def add(k, acc):
                return acc + chip_in[slot, k].astype(F32)

            start = full[slot, chip, mine, :] + core_in[slot, chip]
            ref[...] = lax.fori_loop(1, chips, add, start)

        weight_gradient(ubuf, g_ref[...], put(1))
        core_copy(1).start()

    a0, a1, b0, b1 = stat_end(2)
    coef[4] = both(a0, a1)
    coef[5] = both(b0, b1)
    halo_a, halo_b = halo_both(a0, a1), halo_both(b0, b1)

    def make_dinner(t):
        d = split(delta[at(t), :]) - coef[4][None] - split(inner[at(t), :]) * coef[5][None]
        d = (d * coef[3][None]).reshape(tile, chans)
        pad[pad_at(t), :] = d
        dinn[at(t), :] = d.astype(BF16)

    loop(make_dinner)
    if win is not None:
        chip_start(1)
        weight_gradient(vbuf, dinn[...], put(0))
        core_copy(0).start()
    else:
        weight_gradient(vbuf, dinn[...], put(d1_ref))
    halo_end(2, hc_send, hc_recv)
    sides = [
        ((hc_recv[side] - halo_a - vh_halo[side] * halo_b) * halo_i).astype(BF16)
        for side in range(2)
    ]
    shifts(dbuf, *sides)

    def conv_d(t):
        d = taps(dbuf, w1_ref, t, True) * slope(act_first(t)) * gain1
        delta[at(t), :] = d
        return fold(d), fold(d * vhat_first(t).reshape(tile, chans))

    stat_put(3, *loop_sums(conv_d))
    stat_start(3)
    if win is not None:
        chip_start(0)
    a0, a1, b0, b1 = stat_end(3)
    coef[4] = both(a0, a1)
    coef[5] = both(b0, b1)

    def finish(t):
        d = split(delta[at(t), :]) - coef[4][None] - vhat_first(t) * coef[5][None]
        d = (d * coef[1][None]).reshape(tile, chans)
        out_ref[at(t), :] = (g_ref[at(t), :].astype(F32) + d).astype(BF16)

    loop(finish)
    if win is not None:
        chip_end(1, d2_ref)
        chip_end(0, d1_ref)


def per_device(
    n, scene, grad_out, conv_first, conv_second, gain_first, shift_first, gain_second, shift_second
):
    scenes, height, width, chans = scene.shape
    pixels = scenes * height * width
    win = window(9 * chans, n)
    count = height * width * n * (chans // GROUPS)
    edge_rows = pixels // 8

    def flat(v):
        return jnp.transpose(v, (1, 0, 2, 3)).reshape(pixels, chans)

    params = jnp.concatenate(
        [
            jnp.stack([gain_first, shift_first, gain_second, shift_second]),
            jnp.zeros((4, chans), F32),
        ]
    )
    group = jnp.arange(chans) // (chans // GROUPS)
    mix = (group[:, None] == group[None, :]).astype(F32)
    grad_shape = (9, chans, chans) if win is None else (win[2], chans)
    dma = pltpu.SemaphoreType.DMA
    scratch = [
        pltpu.VMEM((4, 8, chans), F32),
        pltpu.VMEM((4, n, 8, chans), F32),
        pltpu.VMEM((2, 2 * edge_rows, chans), BF16),
        pltpu.VMEM((2, 2 * edge_rows, chans), BF16),
        pltpu.VMEM((2, edge_rows, chans), F32),
        pltpu.VMEM((2, edge_rows, chans), F32),
        pltpu.VMEM((2, edge_rows, chans), F32),
        pltpu.VMEM((2, edge_rows, chans), F32),
        pltpu.VMEM((pixels + 16, chans), F32),
        pltpu.VMEM((3, pixels + 32, chans), BF16),
        pltpu.VMEM((3, pixels + 32, chans), BF16),
        pltpu.VMEM((3, pixels + 32, chans), BF16),
        pltpu.VMEM((3, pixels + 32, chans), BF16),
        pltpu.VMEM((pixels, chans), F32),
        pltpu.VMEM((pixels, chans), F32),
        pltpu.VMEM((pixels, chans), F32),
        pltpu.VMEM((pixels, chans), BF16),
        pltpu.VMEM((6, 16, chans), F32),
        pltpu.VMEM((2, edge_rows, chans), F32),
        dma((4, n)),
        dma((4, n)),
        dma((3, 2)),
        dma((3, 2)),
    ]
    if win is not None:
        own, _, length = win
        chips = n // 2
        scratch += [
            pltpu.VMEM((2, chips, 2 * own, chans), F32),
            pltpu.VMEM((2, chips, length, chans), F32),
            pltpu.VMEM((2, chips, length, chans), BF16),
            pltpu.VMEM((2, chips, length, chans), BF16),
            dma((2,)),
            dma((2,)),
            dma((2, chips)),
            dma((2, chips)),
        ]
    vmem = pl.BlockSpec(memory_space=pltpu.VMEM)
    out, first, second = pl.pallas_call(
        functools.partial(kernel, n, height, count, win),
        out_shape=(
            jax.ShapeDtypeStruct((pixels, chans), BF16),
            jax.ShapeDtypeStruct(grad_shape, F32),
            jax.ShapeDtypeStruct(grad_shape, F32),
        ),
        in_specs=[vmem] * 6,
        out_specs=(vmem, vmem, vmem),
        scratch_shapes=scratch,
        compiler_params=pltpu.CompilerParams(
            collective_id=0, has_side_effects=True, vmem_limit_bytes=56 * 1024 * 1024
        ),
    )(
        flat(scene),
        flat(grad_out),
        conv_first.reshape(9, chans, chans),
        conv_second.reshape(9, chans, chans),
        params,
        mix,
    )
    grad_input = jnp.transpose(out.reshape(height, scenes, width, chans), (1, 0, 2, 3))
    if win is None:
        first, second = (
            lax.psum_scatter(v.reshape(-1), "lon", scatter_dimension=0, tiled=True)
            for v in (first, second)
        )
    else:
        own, off, _ = win
        skip = lax.rem(lax.axis_index("lon"), 2) * (own - off)
        first, second = (
            lax.dynamic_slice_in_dim(v, skip, own, axis=0).reshape(-1) for v in (first, second)
        )
    return grad_input, first, second


def solution(mesh):
    placed = (
        P("groups", None, "lon", None),
        P("groups", None, "lon", None),
        P(),
        P(),
        P(),
        P(),
        P(),
        P(),
    )
    return jax.shard_map(
        functools.partial(per_device, mesh.shape["lon"]),
        mesh=mesh,
        in_specs=placed,
        out_specs=(P("groups", None, "lon", None), P(("groups", "lon")), P(("groups", "lon"))),
        check_vma=False,
    )
```

```python
import functools

import jax
import jax.numpy as jnp
from jax import lax
from jax.experimental import pallas as pl
from jax.experimental.pallas import tpu as pltpu
from jax.sharding import PartitionSpec as P

GROUPS = 32
F32 = jnp.float32
BF16 = jnp.bfloat16
MESH = pl.DeviceIdType.MESH
HIGH = lax.Precision.HIGHEST


def window(rows, n):
    if n % 4 or rows % n or (2 * rows // n) % 8:
        return None
    own = rows // n
    off = own // 8 * 8
    return own, off, 2 * own - off


def sigmoid(a):
    return 1.0 / (1.0 + jnp.exp(-a))


def slope(a):
    sig = sigmoid(a)
    return sig * (1.0 + a * (1.0 - sig))


def kernel(n, height, eps_count, win, *refs):
    (x_raw, g_raw, w1_ref, w2_ref) = refs[:4]
    gain1, shift1, gain2, shift2 = (ref[...] for ref in refs[4:8])
    (out_ref, d1_ref, d2_ref) = refs[8:11]
    (
        st_send, st_recv, ha_send, ha_recv, hb_send, hb_recv, hc_send, hc_recv,
        pad, vbuf, ubuf, gbuf, dbuf, inner, dsil, delta, dinn, coef, vh_halo,
        x_ref, g_ref, mix_ref, st_ss, st_rs, h_ss, h_rs,
    ) = refs[11:37]
    pixels, chans = x_ref.shape
    deep = height // 3
    tile = 16 * deep
    tiles = pixels // tile
    edge_rows = pixels // 8
    me = lax.axis_index("lon")
    right, left = lax.rem(me + 1, n), lax.rem(me + n - 1, n)

    def at(t):
        return pl.ds(pl.multiple_of(t * tile, 16), tile)

    def greet(k, _):
        pl.semaphore_signal(
            barrier, inc=1, device_id={"lon": lax.rem(me + k, n)}, device_id_type=MESH
        )
        return 0

    barrier = pltpu.get_barrier_semaphore()
    lax.fori_loop(1, n, greet, 0)

    def stat_copy(rnd, k):
        return pltpu.make_async_remote_copy(
            src_ref=st_send.at[rnd],
            dst_ref=st_recv.at[rnd, k],
            send_sem=st_ss.at[rnd, k],
            recv_sem=st_rs.at[rnd, k],
            device_id={"lon": lax.rem(me + k, n)},
            device_id_type=MESH,
        )

    def stat_put(rnd, total, second):
        rows = [
            jnp.sum(v[8 * b : 8 * b + 8], axis=0, keepdims=True)
            for v in (total, second)
            for b in range(2)
        ]
        block = jnp.concatenate(rows + [jnp.zeros((4, chans), F32)], axis=0)
        st_send[rnd] = block
        st_recv[rnd, 0] = block

    def stat_start(rnd):
        def go(k, _):
            stat_copy(rnd, k).start()
            return 0

        lax.fori_loop(1, n, go, 0)

    def stat_end(rnd):
        def end(k, _):
            stat_copy(rnd, k).wait()
            return 0

        lax.fori_loop(1, n, end, 0)

        def add(k, acc):
            return acc + st_recv[rnd, k]

        total = lax.fori_loop(1, n, add, st_recv[rnd, 0])
        means = (
            jnp.dot(total, mix_ref[...], precision=HIGH, preferred_element_type=F32)
            * (1.0 / eps_count)
        )
        return [means[r : r + 1] for r in range(4)]

    def halo_copies(rnd, send, recv):
        return [
            pltpu.make_async_remote_copy(
                src_ref=send.at[side],
                dst_ref=recv.at[1 - side],
                send_sem=h_ss.at[rnd, side],
                recv_sem=h_rs.at[rnd, 1 - side],
                device_id={"lon": peer},
                device_id_type=MESH,
            )
            for side, peer in ((0, left), (1, right))
        ]

    def halo_end(rnd, send, recv):
        copies = halo_copies(rnd, send, recv)
        for copy in copies:
            copy.wait_send()
        for copy in copies:
            copy.wait_recv()

    def pick(column, dtype):
        r = lax.broadcasted_iota(jnp.int32, (edge_rows, pixels), 0)
        p = lax.broadcasted_iota(jnp.int32, (edge_rows, pixels), 1)
        return jnp.where(p == 8 * r + column, 1.0, 0.0).astype(dtype)

    def edge(value, column):
        if value.dtype == BF16:
            return jnp.dot(pick(column, BF16), value, preferred_element_type=F32).astype(BF16)
        return jnp.dot(pick(column, F32), value, precision=HIGH, preferred_element_type=F32)

    def both(first, second):
        return jnp.concatenate(
            [jnp.broadcast_to(first, (8, chans)), jnp.broadcast_to(second, (8, chans))], axis=0
        )

    def halo_both(first, second):
        odd = lax.broadcasted_iota(jnp.int32, (edge_rows, chans), 0) & 1
        return jnp.where(odd == 0, first, second)

    def split(v):
        return v.reshape(v.shape[0] // 16, 16, chans)

    def fold(v):
        return jnp.sum(split(v), axis=0)

    def shifts(buf, low, high):
        zero = jnp.zeros((16, chans), BF16)
        for j in range(3):
            buf[j, 0:16] = zero
            buf[j, pixels + 16 : pixels + 32] = zero
        column = lax.broadcasted_iota(jnp.int32, (tile, chans), 0) & 7
        for t in range(tiles):
            p = lax.broadcasted_iota(jnp.int32, (tile, edge_rows), 0) + t * tile
            r = lax.broadcasted_iota(jnp.int32, (tile, edge_rows), 1)
            place = jnp.where((p >> 3) == r, 1.0, 0.0).astype(BF16)
            start = t * tile
            rows = slice(16 + start, 16 + start + tile)
            from_low = jnp.dot(place, low, preferred_element_type=F32)
            from_high = jnp.dot(place, high, preferred_element_type=F32)
            buf[0, rows] = jnp.where(
                column == 0, from_low, pad[start + 7 : start + 7 + tile]
            ).astype(BF16)
            buf[1, rows] = pad[start + 8 : start + 8 + tile].astype(BF16)
            buf[2, rows] = jnp.where(
                column == 7, from_high, pad[start + 9 : start + 9 + tile]
            ).astype(BF16)

    def pad_at(t):
        return pl.ds(pl.multiple_of(t * tile + 8, 8), tile)

    def taps(buf, w_ref, t, transposed):
        acc = jnp.zeros((tile, chans), F32)
        for i in range(3):
            for j in range(3):
                rows = pl.ds(pl.multiple_of(t * tile + 16 * i, 16), tile)
                lhs = buf[j, rows, :]
                if transposed:
                    acc += lax.dot_general(
                        lhs, w_ref[8 - 3 * i - j], (((1,), (1,)), ((), ())),
                        preferred_element_type=F32,
                    )
                else:
                    acc += jnp.dot(lhs, w_ref[3 * i + j], preferred_element_type=F32)
        return acc

    def loop(body):
        def step(t, carry):
            body(t)
            return carry

        lax.fori_loop(0, tiles, step, 0)

    def loop_sums(body):
        zero = jnp.zeros((16, chans), F32)

        def step(t, carry):
            a, b = body(t)
            return carry[0] + a, carry[1] + b

        return lax.fori_loop(0, tiles, step, (zero, zero))

    def member(dim):
        index = lax.broadcasted_iota(jnp.int32, (chans, chans), dim).astype(F32)
        return jnp.floor((index + 0.5) * (GROUPS / chans))

    def rows_of(t):
        return pl.ds(t * deep, deep)

    def gather_rows(raw, t):
        pair = [raw[b, rows_of(t)].astype(F32) for b in range(2)]
        return jnp.concatenate(pair, axis=1)

    def sums_x(t):
        v = gather_rows(x_raw, t).reshape(tile, chans)
        x_ref[at(t), :] = v.astype(BF16)
        g = gather_rows(g_raw, t).reshape(tile, chans)
        g_ref[at(t), :] = g.astype(BF16)
        pad[pad_at(t), :] = g
        return fold(v), fold(v * v)

    stat_put(0, *loop_sums(sums_x))
    for side, column in ((0, 0), (1, 7)):
        ha_send[side, 0:edge_rows] = edge(x_ref[...], column)
        ha_send[side, edge_rows : 2 * edge_rows] = edge(g_ref[...], column)
    pad[0:8] = jnp.zeros((8, chans), F32)
    pad[pixels + 8 : pixels + 16] = jnp.zeros((8, chans), F32)
    pl.semaphore_wait(barrier, n - 1)
    stat_start(0)
    for copy in halo_copies(0, ha_send, ha_recv):
        copy.start()

    mix_ref[...] = jnp.where(member(0) == member(1), 1.0, 0.0)
    halo_end(0, ha_send, ha_recv)
    shifts(gbuf, ha_recv[0, edge_rows : 2 * edge_rows], ha_recv[1, edge_rows : 2 * edge_rows])

    def conv_g(t):
        dsil[at(t), :] = taps(gbuf, w2_ref, t, True)

    loop(conv_g)

    def norm_coefs(rnd):
        m0, m1, q0, q1 = stat_end(rnd)
        i0 = 1.0 / jnp.sqrt(q0 - m0 * m0 + 1e-05)
        i1 = 1.0 / jnp.sqrt(q1 - m1 * m1 + 1e-05)
        return m0, m1, i0, i1

    m0, m1, i0, i1 = norm_coefs(0)
    coef[0] = both(m0, m1)
    coef[1] = both(i0, i1)
    halo_m, halo_i = halo_both(m0, m1), halo_both(i0, i1)

    def vhat_first(t):
        v = split(x_ref[at(t), :].astype(F32))
        return (v - coef[0][None]) * coef[1][None]

    def act_first(t):
        return vhat_first(t).reshape(tile, chans) * gain1 + shift1

    def silu_first(t):
        a = act_first(t)
        pad[pad_at(t), :] = a * sigmoid(a)

    loop(silu_first)
    sides = []
    for side in range(2):
        a = (ha_recv[side, 0:edge_rows].astype(F32) - halo_m) * halo_i * gain1 + shift1
        sides.append((a * sigmoid(a)).astype(BF16))
    shifts(vbuf, *sides)

    def conv_x(t):
        v = taps(vbuf, w1_ref, t, False)
        inner[at(t), :] = v
        return fold(v), fold(v * v)

    stat_put(1, *loop_sums(conv_x))
    stat_start(1)
    hb_send[0] = edge(inner[...], 0)
    hb_send[1] = edge(inner[...], 7)
    for copy in halo_copies(1, hb_send, hb_recv):
        copy.start()

    m0, m1, i0, i1 = norm_coefs(1)
    coef[2] = both(m0, m1)
    coef[3] = both(i0, i1)
    halo_m, halo_i = halo_both(m0, m1), halo_both(i0, i1)

    def second(t):
        vhat = ((split(inner[at(t), :]) - coef[2][None]) * coef[3][None]).reshape(tile, chans)
        inner[at(t), :] = vhat
        a = vhat * gain2 + shift2
        pad[pad_at(t), :] = a * sigmoid(a)
        d = dsil[at(t), :] * slope(a) * gain2
        delta[at(t), :] = d
        return fold(d), fold(d * vhat)

    stat_put(2, *loop_sums(second))
    stat_start(2)
    hc_send[0] = edge(delta[...], 0)
    hc_send[1] = edge(delta[...], 7)
    for copy in halo_copies(2, hc_send, hc_recv):
        copy.start()

    halo_end(1, hb_send, hb_recv)
    sides = []
    for side in range(2):
        vhat = (hb_recv[side] - halo_m) * halo_i
        vh_halo[side] = vhat
        a = vhat * gain2 + shift2
        sides.append((a * sigmoid(a)).astype(BF16))
    shifts(ubuf, *sides)

    def weight_gradient(buf, y, store):
        for i in range(3):
            for j in range(3):
                block = lax.dot_general(
                    buf[j, 16 * i : 16 * i + pixels], y, (((0,), (0,)), ((), ())),
                    preferred_element_type=F32,
                )
                store(3 * i + j, block)

    if win is None:

        def put(ref):
            def store(tap, block):
                ref[tap] = block

            return store

        weight_gradient(ubuf, g_ref[...], put(d2_ref))
    else:
        (full, core_in, pair_out, pair_in, chip_out, chip_in, c_ss, c_rs, p_ss, p_rs, q_ss, q_rs) = (
            refs[37:]
        )
        own, off, length = win
        chips = n // 2
        pairs = chips // 2
        chip, core = me // 2, lax.rem(me, 2)
        row, side_of = chip // 2, lax.rem(chip, 2)
        mine = pl.ds(pl.multiple_of(off * core, 8), length)
        other = pl.ds(pl.multiple_of(off * (1 - core), 8), length)

        def put(slot):
            def store(tap, block):
                row = tap * chans
                while row < (tap + 1) * chans:
                    q, r = divmod(row, 2 * own)
                    stop = min((tap + 1) * chans, (q + 1) * 2 * own)
                    low = row - tap * chans
                    full[slot, q, r : r + stop - row] = block[low : low + stop - row]
                    row = stop

            return store

        def core_copy(slot):
            return pltpu.make_async_remote_copy(
                src_ref=full.at[slot, :, other, :],
                dst_ref=core_in.at[slot],
                send_sem=c_ss.at[slot],
                recv_sem=c_rs.at[slot],
                device_id={"lon": me + 1 - 2 * core},
                device_id_type=MESH,
            )

        def pair_copy(slot, k):
            return pltpu.make_async_remote_copy(
                src_ref=pair_out.at[slot, k],
                dst_ref=pair_in.at[slot, k],
                send_sem=p_ss.at[slot, k],
                recv_sem=p_rs.at[slot, k],
                device_id={"lon": 2 * (chip + 1 - 2 * side_of) + core},
                device_id_type=MESH,
            )

        def chip_copy(slot, k):
            to = 2 * lax.rem(row + k, pairs) + side_of
            return pltpu.make_async_remote_copy(
                src_ref=chip_out.at[slot, k],
                dst_ref=chip_in.at[slot, k],
                send_sem=q_ss.at[slot, k],
                recv_sem=q_rs.at[slot, k],
                device_id={"lon": 2 * to + core},
                device_id_type=MESH,
            )

        def pair_start(slot):
            core_copy(slot).wait()

            def go(k, _):
                to = 2 * lax.rem(row + k, pairs) + 1 - side_of
                pair_out[slot, k - 1] = (
                    full[slot, to, mine, :] + core_in[slot, to]
                ).astype(BF16)
                pair_copy(slot, k - 1).start()
                return 0

            lax.fori_loop(1, pairs + 1, go, 0)

        def pair_sum(slot, k):
            to = 2 * lax.rem(row + k, pairs) + side_of
            pair_copy(slot, k - 1).wait()
            return full[slot, to, mine, :] + core_in[slot, to] + pair_in[slot, k - 1].astype(F32)

        def chip_start(slot):
            def go(k, _):
                chip_out[slot, k] = pair_sum(slot, k).astype(BF16)
                chip_copy(slot, k).start()
                return 0

            lax.fori_loop(1, pairs, go, 0)

        def chip_end(slot, ref):
            def add(k, acc):
                chip_copy(slot, k).wait()
                return acc + chip_in[slot, k].astype(F32)

            total = lax.fori_loop(1, pairs, add, pair_sum(slot, pairs))
            skip = own - off
            ref[...] = jnp.where(core == 0, total[0:own], total[skip : skip + own])

        weight_gradient(ubuf, g_ref[...], put(1))
        core_copy(1).start()

    a0, a1, b0, b1 = stat_end(2)
    coef[4] = both(a0, a1)
    coef[5] = both(b0, b1)
    halo_a, halo_b = halo_both(a0, a1), halo_both(b0, b1)

    def make_dinner(t):
        d = split(delta[at(t), :]) - coef[4][None] - split(inner[at(t), :]) * coef[5][None]
        d = (d * coef[3][None]).reshape(tile, chans)
        pad[pad_at(t), :] = d
        dinn[at(t), :] = d.astype(BF16)

    loop(make_dinner)
    if win is not None:
        pair_start(1)
        weight_gradient(vbuf, dinn[...], put(0))
        core_copy(0).start()
    else:
        weight_gradient(vbuf, dinn[...], put(d1_ref))
    halo_end(2, hc_send, hc_recv)
    sides = [
        ((hc_recv[side] - halo_a - vh_halo[side] * halo_b) * halo_i).astype(BF16)
        for side in range(2)
    ]
    shifts(dbuf, *sides)
    if win is not None:
        chip_start(1)
        pair_start(0)

    def conv_d(t):
        d = taps(dbuf, w1_ref, t, True) * slope(act_first(t)) * gain1
        delta[at(t), :] = d
        return fold(d), fold(d * vhat_first(t).reshape(tile, chans))

    stat_put(3, *loop_sums(conv_d))
    stat_start(3)
    if win is not None:
        chip_start(0)
    a0, a1, b0, b1 = stat_end(3)
    coef[4] = both(a0, a1)
    coef[5] = both(b0, b1)

    def finish(t):
        d = split(delta[at(t), :]) - coef[4][None] - vhat_first(t) * coef[5][None]
        d = d * coef[1][None] + split(g_ref[at(t), :].astype(F32))
        for b in range(2):
            out_ref[b, rows_of(t)] = d[:, 8 * b : 8 * b + 8].astype(BF16)

    loop(finish)
    if win is not None:
        chip_end(1, d2_ref)
        chip_end(0, d1_ref)


def per_device(
    n, scene, grad_out, conv_first, conv_second, gain_first, shift_first, gain_second, shift_second
):
    scenes, height, width, chans = scene.shape
    pixels = scenes * height * width
    win = window(9 * chans, n)
    count = height * width * n * (chans // GROUPS)
    edge_rows = pixels // 8

    grad_shape = (9, chans, chans) if win is None else (win[0], chans)
    dma = pltpu.SemaphoreType.DMA
    scratch = [
        pltpu.VMEM((4, 8, chans), F32),
        pltpu.VMEM((4, n, 8, chans), F32),
        pltpu.VMEM((2, 2 * edge_rows, chans), BF16),
        pltpu.VMEM((2, 2 * edge_rows, chans), BF16),
        pltpu.VMEM((2, edge_rows, chans), F32),
        pltpu.VMEM((2, edge_rows, chans), F32),
        pltpu.VMEM((2, edge_rows, chans), F32),
        pltpu.VMEM((2, edge_rows, chans), F32),
        pltpu.VMEM((pixels + 16, chans), F32),
        pltpu.VMEM((3, pixels + 32, chans), BF16),
        pltpu.VMEM((3, pixels + 32, chans), BF16),
        pltpu.VMEM((3, pixels + 32, chans), BF16),
        pltpu.VMEM((3, pixels + 32, chans), BF16),
        pltpu.VMEM((pixels, chans), F32),
        pltpu.VMEM((pixels, chans), F32),
        pltpu.VMEM((pixels, chans), F32),
        pltpu.VMEM((pixels, chans), BF16),
        pltpu.VMEM((6, 16, chans), F32),
        pltpu.VMEM((2, edge_rows, chans), F32),
        pltpu.VMEM((pixels, chans), BF16),
        pltpu.VMEM((pixels, chans), BF16),
        pltpu.VMEM((chans, chans), F32),
        dma((4, n)),
        dma((4, n)),
        dma((3, 2)),
        dma((3, 2)),
    ]
    if win is not None:
        own, _, length = win
        chips = n // 2
        pairs = chips // 2
        scratch += [
            pltpu.VMEM((2, chips, 2 * own, chans), F32),
            pltpu.VMEM((2, chips, length, chans), F32),
            pltpu.VMEM((2, pairs, length, chans), BF16),
            pltpu.VMEM((2, pairs, length, chans), BF16),
            pltpu.VMEM((2, pairs, length, chans), BF16),
            pltpu.VMEM((2, pairs, length, chans), BF16),
            dma((2,)),
            dma((2,)),
            dma((2, pairs)),
            dma((2, pairs)),
            dma((2, pairs)),
            dma((2, pairs)),
        ]
    vmem = pl.BlockSpec(memory_space=pltpu.VMEM)
    out, first, second = pl.pallas_call(
        functools.partial(kernel, n, height, count, win),
        out_shape=(
            jax.ShapeDtypeStruct(scene.shape, BF16),
            jax.ShapeDtypeStruct(grad_shape, F32),
            jax.ShapeDtypeStruct(grad_shape, F32),
        ),
        in_specs=[vmem] * 8,
        out_specs=(vmem, vmem, vmem),
        scratch_shapes=scratch,
        compiler_params=pltpu.CompilerParams(
            collective_id=0, has_side_effects=True, vmem_limit_bytes=56 * 1024 * 1024
        ),
    )(
        scene,
        grad_out,
        conv_first.reshape(9, chans, chans),
        conv_second.reshape(9, chans, chans),
        *(v.reshape(1, chans) for v in (gain_first, shift_first, gain_second, shift_second)),
    )
    if win is None:
        first, second = (
            lax.psum_scatter(v.reshape(-1), "lon", scatter_dimension=0, tiled=True)
            for v in (first, second)
        )
    return out, first.reshape(-1), second.reshape(-1)


def solution(mesh):
    placed = (
        P("groups", None, "lon", None),
        P("groups", None, "lon", None),
        P(),
        P(),
        P(),
        P(),
        P(),
        P(),
    )
    return jax.shard_map(
        functools.partial(per_device, mesh.shape["lon"]),
        mesh=mesh,
        in_specs=placed,
        out_specs=(P("groups", None, "lon", None), P(("groups", "lon")), P(("groups", "lon"))),
        check_vma=False,
    )
```

```python
import functools

import jax
import jax.numpy as jnp
from jax import lax
from jax.experimental import pallas as pl
from jax.experimental.pallas import tpu as pltpu
from jax.sharding import PartitionSpec as P

GROUPS = 32
F32 = jnp.float32
BF16 = jnp.bfloat16
MESH = pl.DeviceIdType.MESH


def window(rows, n):
    if n % 4 or rows % n or (2 * rows // n) % 8:
        return None
    own = rows // n
    off = own // 8 * 8
    return own, off, 2 * own - off


def sigmoid(a):
    return 1.0 / (1.0 + jnp.exp(-a))


def slope(a):
    sig = sigmoid(a)
    return sig * (1.0 + a * (1.0 - sig))


def kernel(n, height, eps_count, win, *refs):
    (x_raw, g_raw, w1_hbm, w2_hbm) = refs[:4]
    gain1, shift1, gain2, shift2 = (ref[...].reshape(1, -1) for ref in refs[4:8])
    (out_ref, d1_ref, d2_ref) = refs[8:11]
    (
        st_send, st_recv, ha_send, ha_recv, hb_send, hb_recv, hc_send, hc_recv,
        pad, vbuf, ubuf, gbuf, dbuf, inner, dsil, delta, dinn, coef, vh_halo,
        x_ref, g_ref, mix_ref, w1_ref, w2_ref, w_sems, st_ss, st_rs, h_ss, h_rs,
    ) = refs[11:40]
    pixels, chans = x_ref.shape
    deep = height // 3
    tile = 16 * deep
    tiles = pixels // tile
    edge_rows = pixels // 8
    me = lax.axis_index("lon")
    right, left = lax.rem(me + 1, n), lax.rem(me + n - 1, n)

    def at(t):
        return pl.ds(pl.multiple_of(t * tile, 16), tile)

    def greet(k, _):
        pl.semaphore_signal(
            barrier, inc=1, device_id={"lon": lax.rem(me + k, n)}, device_id_type=MESH
        )
        return 0

    fetch_first = pltpu.make_async_copy(w1_hbm, w1_ref, w_sems.at[0])
    fetch_second = pltpu.make_async_copy(w2_hbm, w2_ref, w_sems.at[1])
    barrier = pltpu.get_barrier_semaphore()
    fetch_second.start()
    fetch_first.start()
    lax.fori_loop(1, n, greet, 0)

    def stat_copy(rnd, k):
        return pltpu.make_async_remote_copy(
            src_ref=st_send.at[rnd],
            dst_ref=st_recv.at[rnd, k],
            send_sem=st_ss.at[rnd, k],
            recv_sem=st_rs.at[rnd, k],
            device_id={"lon": lax.rem(me + k, n)},
            device_id_type=MESH,
        )

    def stat_put(rnd, total, second):
        rows = [
            jnp.sum(v[8 * b : 8 * b + 8], axis=0, keepdims=True)
            for v in (total, second)
            for b in range(2)
        ]
        block = jnp.concatenate(rows + [jnp.zeros((4, chans), F32)], axis=0)
        st_send[rnd] = block
        st_recv[rnd, 0] = block

    def stat_start(rnd):
        def go(k, _):
            stat_copy(rnd, k).start()
            return 0

        lax.fori_loop(1, n, go, 0)

    def stat_end(rnd):
        def end(k, _):
            stat_copy(rnd, k).wait()
            return 0

        lax.fori_loop(1, n, end, 0)

        def add(k, acc):
            return acc + st_recv[rnd, k]

        total = lax.fori_loop(1, n, add, st_recv[rnd, 0])
        high = total.astype(BF16)
        rest = total - high.astype(F32)
        middle = rest.astype(BF16)
        low = (rest - middle.astype(F32)).astype(BF16)
        means = sum(
            jnp.dot(piece, mix_ref[...], preferred_element_type=F32)
            for piece in (low, middle, high)
        ) * (1.0 / eps_count)
        return [means[r : r + 1] for r in range(4)]

    def halo_copies(rnd, send, recv):
        return [
            pltpu.make_async_remote_copy(
                src_ref=send.at[side],
                dst_ref=recv.at[1 - side],
                send_sem=h_ss.at[rnd, side],
                recv_sem=h_rs.at[rnd, 1 - side],
                device_id={"lon": peer},
                device_id_type=MESH,
            )
            for side, peer in ((0, left), (1, right))
        ]

    def halo_end(rnd, send, recv):
        copies = halo_copies(rnd, send, recv)
        for copy in copies:
            copy.wait_send()
        for copy in copies:
            copy.wait_recv()

    def edge(ref, column, start=0):
        tiles_of_eight = ref[start : start + pixels].reshape(edge_rows, 8, chans)
        return tiles_of_eight[:, column, :]

    def both(first, second):
        return jnp.concatenate(
            [jnp.broadcast_to(first, (8, chans)), jnp.broadcast_to(second, (8, chans))], axis=0
        )

    def halo_both(first, second):
        odd = lax.broadcasted_iota(jnp.int32, (edge_rows, chans), 0) & 1
        return jnp.where(odd == 0, first, second)

    def split(v):
        return v.reshape(v.shape[0] // 16, 16, chans)

    def fold(v):
        return jnp.sum(split(v), axis=0)

    def shifts(buf, low, high):
        zero = jnp.zeros((16, chans), BF16)
        for j in range(3):
            buf[j, 0:16] = zero
            buf[j, pixels + 16 : pixels + 32] = zero
        column = lax.broadcasted_iota(jnp.int32, (tile, chans), 0) & 7
        for t in range(tiles):
            p = lax.broadcasted_iota(jnp.int32, (tile, edge_rows), 0) + t * tile
            r = lax.broadcasted_iota(jnp.int32, (tile, edge_rows), 1)
            place = jnp.where((p >> 3) == r, 1.0, 0.0).astype(BF16)
            start = t * tile
            rows = slice(16 + start, 16 + start + tile)
            from_low = jnp.dot(place, low, preferred_element_type=F32)
            from_high = jnp.dot(place, high, preferred_element_type=F32)
            buf[0, rows] = jnp.where(
                column == 0, from_low, pad[start + 7 : start + 7 + tile]
            ).astype(BF16)
            buf[1, rows] = pad[start + 8 : start + 8 + tile].astype(BF16)
            buf[2, rows] = jnp.where(
                column == 7, from_high, pad[start + 9 : start + 9 + tile]
            ).astype(BF16)

    def pad_at(t):
        return pl.ds(pl.multiple_of(t * tile + 8, 8), tile)

    def taps(buf, w_ref, t, transposed):
        acc = jnp.zeros((tile, chans), F32)
        for i in range(3):
            for j in range(3):
                rows = pl.ds(pl.multiple_of(t * tile + 16 * i, 16), tile)
                lhs = buf[j, rows, :]
                if transposed:
                    acc += lax.dot_general(
                        lhs, w_ref[8 - 3 * i - j], (((1,), (1,)), ((), ())),
                        preferred_element_type=F32,
                    )
                else:
                    acc += jnp.dot(lhs, w_ref[3 * i + j], preferred_element_type=F32)
        return acc

    def loop(body):
        def step(t, carry):
            body(t)
            return carry

        lax.fori_loop(0, tiles, step, 0)

    def loop_sums(body, between=None):
        zero = jnp.zeros((16, chans), F32)
        if between is not None:
            partial = lax.fori_loop(
                0, tiles - 1, lambda t, c: tuple(x + y for x, y in zip(c, body(t))), (zero, zero)
            )
            between()
            return tuple(x + y for x, y in zip(partial, body(tiles - 1)))

        def step(t, carry):
            a, b = body(t)
            return carry[0] + a, carry[1] + b

        return lax.fori_loop(0, tiles, step, (zero, zero))

    def member(dim):
        index = lax.broadcasted_iota(jnp.int32, (chans, chans), dim).astype(F32)
        return jnp.floor((index + 0.5) * (GROUPS / chans))

    def rows_of(t):
        return pl.ds(t * deep, deep)

    def gather_rows(raw, t):
        pair = [raw[b, rows_of(t)].astype(F32) for b in range(2)]
        return jnp.concatenate(pair, axis=1)

    def sums_x(t):
        v = gather_rows(x_raw, t).reshape(tile, chans)
        x_ref[at(t), :] = v.astype(BF16)
        delta[at(t), :] = v
        g = gather_rows(g_raw, t).reshape(tile, chans)
        g_ref[at(t), :] = g.astype(BF16)
        pad[pad_at(t), :] = g
        return fold(v), fold(v * v)

    stat_put(0, *loop_sums(sums_x))
    for side, column in ((0, 0), (1, 7)):
        ha_send[side, 0:edge_rows] = edge(delta, column).astype(BF16)
        ha_send[side, edge_rows : 2 * edge_rows] = edge(pad, column, 8).astype(BF16)
    pad[0:8] = jnp.zeros((8, chans), F32)
    pad[pixels + 8 : pixels + 16] = jnp.zeros((8, chans), F32)
    pl.semaphore_wait(barrier, n - 1)
    stat_start(0)
    for copy in halo_copies(0, ha_send, ha_recv):
        copy.start()

    mix_ref[...] = jnp.where(member(0) == member(1), 1.0, 0.0).astype(BF16)
    halo_end(0, ha_send, ha_recv)
    shifts(gbuf, ha_recv[0, edge_rows : 2 * edge_rows], ha_recv[1, edge_rows : 2 * edge_rows])

    def conv_g(t):
        dsil[at(t), :] = taps(gbuf, w2_ref, t, True)

    fetch_second.wait()
    loop(conv_g)

    def norm_coefs(rnd):
        m0, m1, q0, q1 = stat_end(rnd)
        i0 = 1.0 / jnp.sqrt(q0 - m0 * m0 + 1e-05)
        i1 = 1.0 / jnp.sqrt(q1 - m1 * m1 + 1e-05)
        return m0, m1, i0, i1

    m0, m1, i0, i1 = norm_coefs(0)
    coef[0] = both(m0, m1)
    coef[1] = both(i0, i1)
    halo_m, halo_i = halo_both(m0, m1), halo_both(i0, i1)

    def vhat_first(t):
        v = split(x_ref[at(t), :].astype(F32))
        return (v - coef[0][None]) * coef[1][None]

    def act_first(t):
        return vhat_first(t).reshape(tile, chans) * gain1 + shift1

    def silu_first(t):
        a = act_first(t)
        pad[pad_at(t), :] = a * sigmoid(a)

    loop(silu_first)
    sides = []
    for side in range(2):
        a = (ha_recv[side, 0:edge_rows].astype(F32) - halo_m) * halo_i * gain1 + shift1
        sides.append((a * sigmoid(a)).astype(BF16))
    shifts(vbuf, *sides)

    def conv_x(t):
        v = taps(vbuf, w1_ref, t, False)
        inner[at(t), :] = v
        return fold(v), fold(v * v)

    fetch_first.wait()
    stat_put(1, *loop_sums(conv_x))
    stat_start(1)
    hb_send[0] = edge(inner, 0)
    hb_send[1] = edge(inner, 7)
    for copy in halo_copies(1, hb_send, hb_recv):
        copy.start()

    m0, m1, i0, i1 = norm_coefs(1)
    coef[2] = both(m0, m1)
    coef[3] = both(i0, i1)
    halo_m, halo_i = halo_both(m0, m1), halo_both(i0, i1)

    def second(t):
        vhat = ((split(inner[at(t), :]) - coef[2][None]) * coef[3][None]).reshape(tile, chans)
        inner[at(t), :] = vhat
        a = vhat * gain2 + shift2
        pad[pad_at(t), :] = a * sigmoid(a)
        d = dsil[at(t), :] * slope(a) * gain2
        delta[at(t), :] = d
        return fold(d), fold(d * vhat)

    stat_put(2, *loop_sums(second))
    stat_start(2)
    hc_send[0] = edge(delta, 0)
    hc_send[1] = edge(delta, 7)
    for copy in halo_copies(2, hc_send, hc_recv):
        copy.start()

    halo_end(1, hb_send, hb_recv)
    sides = []
    for side in range(2):
        vhat = (hb_recv[side] - halo_m) * halo_i
        vh_halo[side] = vhat
        a = vhat * gain2 + shift2
        sides.append((a * sigmoid(a)).astype(BF16))
    shifts(ubuf, *sides)

    def weight_gradient(buf, y, store):
        for i in range(3):
            for j in range(3):
                block = lax.dot_general(
                    buf[j, 16 * i : 16 * i + pixels], y, (((0,), (0,)), ((), ())),
                    preferred_element_type=F32,
                )
                store(3 * i + j, block)

    if win is None:

        def put(ref):
            def store(tap, block):
                ref[tap] = block

            return store

        weight_gradient(ubuf, g_ref[...], put(d2_ref))
    else:
        (full, core_in, pair_out, pair_in, chip_out, chip_in, c_ss, c_rs, p_ss, p_rs, q_ss, q_rs) = (
            refs[40:]
        )
        own, off, length = win
        chips = n // 2
        pairs = chips // 2
        chip, core = me // 2, lax.rem(me, 2)
        row, side_of = chip // 2, lax.rem(chip, 2)
        mine = pl.ds(pl.multiple_of(off * core, 8), length)
        other = pl.ds(pl.multiple_of(off * (1 - core), 8), length)

        def put(slot):
            def store(tap, block):
                row = tap * chans
                while row < (tap + 1) * chans:
                    q, r = divmod(row, 2 * own)
                    stop = min((tap + 1) * chans, (q + 1) * 2 * own)
                    low = row - tap * chans
                    full[slot, q, r : r + stop - row] = block[low : low + stop - row]
                    row = stop

            return store

        def core_copy(slot):
            return pltpu.make_async_remote_copy(
                src_ref=full.at[slot, :, other, :],
                dst_ref=core_in.at[slot],
                send_sem=c_ss.at[slot],
                recv_sem=c_rs.at[slot],
                device_id={"lon": me + 1 - 2 * core},
                device_id_type=MESH,
            )

        def pair_copy(slot, k):
            return pltpu.make_async_remote_copy(
                src_ref=pair_out.at[slot, k],
                dst_ref=pair_in.at[slot, k],
                send_sem=p_ss.at[slot, k],
                recv_sem=p_rs.at[slot, k],
                device_id={"lon": 2 * (chip + 1 - 2 * side_of) + core},
                device_id_type=MESH,
            )

        def chip_copy(slot, k):
            to = 2 * lax.rem(row + k, pairs) + side_of
            return pltpu.make_async_remote_copy(
                src_ref=chip_out.at[slot, k],
                dst_ref=chip_in.at[slot, k],
                send_sem=q_ss.at[slot, k],
                recv_sem=q_rs.at[slot, k],
                device_id={"lon": 2 * to + core},
                device_id_type=MESH,
            )

        def pair_start(slot):
            core_copy(slot).wait()

            def go(k, _):
                to = 2 * lax.rem(row + k, pairs) + 1 - side_of
                pair_out[slot, k - 1] = (
                    full[slot, to, mine, :] + core_in[slot, to]
                ).astype(BF16)
                pair_copy(slot, k - 1).start()
                return 0

            lax.fori_loop(1, pairs + 1, go, 0)

        def pair_sum(slot, k):
            to = 2 * lax.rem(row + k, pairs) + side_of
            pair_copy(slot, k - 1).wait()
            return full[slot, to, mine, :] + core_in[slot, to] + pair_in[slot, k - 1].astype(F32)

        def chip_start(slot):
            def go(k, _):
                chip_out[slot, k] = pair_sum(slot, k).astype(BF16)
                chip_copy(slot, k).start()
                return 0

            lax.fori_loop(1, pairs, go, 0)

        def chip_end(slot, ref):
            def add(k, acc):
                chip_copy(slot, k).wait()
                return acc + chip_in[slot, k].astype(F32)

            total = lax.fori_loop(1, pairs, add, pair_sum(slot, pairs))
            skip = own - off
            ref[...] = jnp.where(core == 0, total[0:own], total[skip : skip + own])

        weight_gradient(ubuf, g_ref[...], put(1))
        core_copy(1).start()

    a0, a1, b0, b1 = stat_end(2)
    coef[4] = both(a0, a1)
    coef[5] = both(b0, b1)
    halo_a, halo_b = halo_both(a0, a1), halo_both(b0, b1)

    def make_dinner(t):
        d = split(delta[at(t), :]) - coef[4][None] - split(inner[at(t), :]) * coef[5][None]
        d = (d * coef[3][None]).reshape(tile, chans)
        pad[pad_at(t), :] = d
        dinn[at(t), :] = d.astype(BF16)

    loop(make_dinner)
    if win is not None:
        pair_start(1)
        weight_gradient(vbuf, dinn[...], put(0))
        core_copy(0).start()
    else:
        weight_gradient(vbuf, dinn[...], put(d1_ref))
    halo_end(2, hc_send, hc_recv)
    sides = [
        ((hc_recv[side] - halo_a - vh_halo[side] * halo_b) * halo_i).astype(BF16)
        for side in range(2)
    ]
    shifts(dbuf, *sides)

    def conv_d(t):
        d = taps(dbuf, w1_ref, t, True) * slope(act_first(t)) * gain1
        delta[at(t), :] = d
        return fold(d), fold(d * vhat_first(t).reshape(tile, chans))

    def between():
        if win is not None:
            chip_start(1)
            pair_start(0)

    stat_put(3, *loop_sums(conv_d, between))
    stat_start(3)
    if win is not None:
        chip_start(0)
    a0, a1, b0, b1 = stat_end(3)
    coef[4] = both(a0, a1)
    coef[5] = both(b0, b1)

    def finish(t):
        d = split(delta[at(t), :]) - coef[4][None] - vhat_first(t) * coef[5][None]
        d = d * coef[1][None] + split(g_ref[at(t), :].astype(F32))
        for b in range(2):
            out_ref[b, rows_of(t)] = d[:, 8 * b : 8 * b + 8].astype(BF16)

    loop(finish)
    if win is not None:
        chip_end(1, d2_ref)
        chip_end(0, d1_ref)


def per_device(
    n, scene, grad_out, conv_first, conv_second, gain_first, shift_first, gain_second, shift_second
):
    scenes, height, width, chans = scene.shape
    pixels = scenes * height * width
    win = window(9 * chans, n)
    count = height * width * n * (chans // GROUPS)
    edge_rows = pixels // 8

    grad_shape = (9, chans, chans) if win is None else (win[0], chans)
    dma = pltpu.SemaphoreType.DMA
    scratch = [
        pltpu.VMEM((4, 8, chans), F32),
        pltpu.VMEM((4, n, 8, chans), F32),
        pltpu.VMEM((2, 2 * edge_rows, chans), BF16),
        pltpu.VMEM((2, 2 * edge_rows, chans), BF16),
        pltpu.VMEM((2, edge_rows, chans), F32),
        pltpu.VMEM((2, edge_rows, chans), F32),
        pltpu.VMEM((2, edge_rows, chans), F32),
        pltpu.VMEM((2, edge_rows, chans), F32),
        pltpu.VMEM((pixels + 16, chans), F32),
        pltpu.VMEM((3, pixels + 32, chans), BF16),
        pltpu.VMEM((3, pixels + 32, chans), BF16),
        pltpu.VMEM((3, pixels + 32, chans), BF16),
        pltpu.VMEM((3, pixels + 32, chans), BF16),
        pltpu.VMEM((pixels, chans), F32),
        pltpu.VMEM((pixels, chans), F32),
        pltpu.VMEM((pixels, chans), F32),
        pltpu.VMEM((pixels, chans), BF16),
        pltpu.VMEM((6, 16, chans), F32),
        pltpu.VMEM((2, edge_rows, chans), F32),
        pltpu.VMEM((pixels, chans), BF16),
        pltpu.VMEM((pixels, chans), BF16),
        pltpu.VMEM((chans, chans), BF16),
        pltpu.VMEM((9, chans, chans), BF16),
        pltpu.VMEM((9, chans, chans), BF16),
        dma((2,)),
        dma((4, n)),
        dma((4, n)),
        dma((3, 2)),
        dma((3, 2)),
    ]
    if win is not None:
        own, _, length = win
        chips = n // 2
        pairs = chips // 2
        scratch += [
            pltpu.VMEM((2, chips, 2 * own, chans), F32),
            pltpu.VMEM((2, chips, length, chans), F32),
            pltpu.VMEM((2, pairs, length, chans), BF16),
            pltpu.VMEM((2, pairs, length, chans), BF16),
            pltpu.VMEM((2, pairs, length, chans), BF16),
            pltpu.VMEM((2, pairs, length, chans), BF16),
            dma((2,)),
            dma((2,)),
            dma((2, pairs)),
            dma((2, pairs)),
            dma((2, pairs)),
            dma((2, pairs)),
        ]
    vmem = pl.BlockSpec(memory_space=pltpu.VMEM)
    out, first, second = pl.pallas_call(
        functools.partial(kernel, n, height, count, win),
        out_shape=(
            jax.ShapeDtypeStruct(scene.shape, BF16),
            jax.ShapeDtypeStruct(grad_shape, F32),
            jax.ShapeDtypeStruct(grad_shape, F32),
        ),
        in_specs=[vmem] * 2 + [pl.BlockSpec(memory_space=pl.ANY)] * 2 + [vmem] * 4,
        out_specs=(vmem, vmem, vmem),
        scratch_shapes=scratch,
        compiler_params=pltpu.CompilerParams(
            collective_id=0, has_side_effects=True, vmem_limit_bytes=56 * 1024 * 1024
        ),
    )(
        scene,
        grad_out,
        conv_first.reshape(9, chans, chans),
        conv_second.reshape(9, chans, chans),
        gain_first,
        shift_first,
        gain_second,
        shift_second,
    )
    if win is None:
        first, second = (
            lax.psum_scatter(v.reshape(-1), "lon", scatter_dimension=0, tiled=True)
            for v in (first, second)
        )
    return out, first.reshape(-1), second.reshape(-1)


def solution(mesh):
    placed = (
        P("groups", None, "lon", None),
        P("groups", None, "lon", None),
        P(),
        P(),
        P(),
        P(),
        P(),
        P(),
    )
    return jax.shard_map(
        functools.partial(per_device, mesh.shape["lon"]),
        mesh=mesh,
        in_specs=placed,
        out_specs=(P("groups", None, "lon", None), P(("groups", "lon")), P(("groups", "lon"))),
        check_vma=False,
    )
```
